128 devices in a mesh: vel: 4 (over y_lo, core), pos: 32 (over y_hi, z, x).
Axes of the slice: x: 4, y: 4 (y_hi: 2, y_lo: 2; y = y_hi * 2 + y_lo), z: 4, core: 2. Of those that a mesh axis runs over, the one named last changes fastest.
Arguments:
- value_next: float32 [64, 64, 64, 512], P('pos', 'vel'), may hold values from -6 to 6
- density: float32 [64, 64, 64, 512], P('pos', 'vel'), as said below
Outputs:
- value_now: float32 [64, 64, 64, 512], P('pos', 'vel')
- density_next: float32 [64, 64, 64, 512], P('pos', 'vel')
The draws below stay inside these ranges and needn't reach their ends.
Inputs may be any that keep to these rules, and one draw needn't show every extreme that they name: density is positive everywhere.
All inputs are finite; a program needn't handle non-finite values.
Results may differ from the reference program's by a relative error of at most 0.00002.
Values sent between devices are 32-bit elements; how exact they have to be, the bound alone decides.
A program may use at most 192 MiB of HBM per device.

```python
import math
import jax
import jax.numpy as jnp
from jax import lax

NV = 64
NY = 512
NX = 64


def draw_density(key, part):
    first, second, third = jax.random.split(key, 3)
    rising = 10.0 ** (jnp.arange(NV, dtype=jnp.float32) / (NV - 1))
    column_scale = jnp.exp(jax.random.uniform(first, (NV,), jnp.float32, 0.0, math.log(10.0)))
    noise = jax.random.uniform(second, (NX, NV, NV, NY), jnp.float32, 0.5, 1.5)
    place = jnp.exp(jax.random.uniform(third, (NX, NY), jnp.float32, math.log(0.3), math.log(3.0)))
    result = place[:, None, None, :] * rising[None, :, None, None] * column_scale[None, None, :, None] * noise / 15.0
    return result.astype(jnp.float32)


def block_scale(key, extent, cuts, smallest, high):
    level = 1.0
    for axis_at, blocks in cuts:
        heights = jax.random.uniform(jax.random.fold_in(jax.random.fold_in(key, 6), axis_at), (blocks,), jnp.float32, smallest / len(cuts), high / len(cuts))
        level = level * jnp.repeat(jnp.exp(heights), extent[axis_at] // blocks).reshape((-1,) + (1,) * (len(extent) - 1 - axis_at))
    return level


def bell_draw(rng, dims, width, limit, cuts=(), kind=jnp.bfloat16):
    values = width * jax.random.normal(rng, dims, jnp.float32)
    if cuts:
        values = values * block_scale(rng, dims, cuts, -0.22, 0.18)
    return jnp.clip(values, -limit, limit).astype(kind)


def setup_inputs(seed: int = 0) -> dict:
    streams_of = jax.random.split(jax.random.key(seed), 3)
    value_next = bell_draw(streams_of[0], (NX, NV, NV, NY), 1.0, 6.0, ((0, 32), (1, 4)), jnp.float32)
    density = draw_density(jax.random.fold_in(streams_of[2], 71), 0)
    return {"value_next": value_next, "density": density}


COURANT = 0.4
CONTROL_COST = 0.25
VISCOSITY = 0.15
CROWDING = 0.3


def speeds(first, count, total):
    index = first + jnp.arange(count, dtype=jnp.int32)
    return COURANT * ((index.astype(jnp.float32) + 0.5 - total / 2) / (total / 2))


def along_second(array, step):
    rolled = jnp.roll(array, -step, 2)
    place = lax.broadcasted_iota(jnp.int32, array.shape, 2)
    edge = array.shape[2] - 1 if step > 0 else 0
    return jnp.where(place == edge, array, rolled)


def value_core(centre, x_up, x_dn, a_up, a_dn, speed_x, speed_y, crowding):
    along_x = speed_x[None, :, None, None]
    along_y = speed_y[None, None, :, None]
    carry_x = jnp.where(along_x > 0, along_x * (x_up - centre), along_x * (centre - x_dn))
    ahead_y = jnp.roll(centre, -1, 3) - centre
    behind_y = centre - jnp.roll(centre, 1, 3)
    carry_y = jnp.where(along_y > 0, along_y * ahead_y, along_y * behind_y)
    upper_v = a_up - centre
    lower_v = centre - a_dn
    upper_w = along_second(centre, 1) - centre
    lower_w = centre - along_second(centre, -1)
    hamilton = 0.5 * (jnp.square(jnp.maximum(lower_v, 0.0)) + jnp.square(jnp.minimum(upper_v, 0.0))
                      + jnp.square(jnp.maximum(lower_w, 0.0)) + jnp.square(jnp.minimum(upper_w, 0.0)))
    laplace = upper_v - lower_v + upper_w - lower_w
    return centre + carry_x + carry_y - CONTROL_COST * hamilton + VISCOSITY * laplace + crowding[:, None, None, :]


def density_core(centre, x_up, x_dn, a_up, a_dn, control, control_up, control_dn, speed_x, speed_y):
    along_x = speed_x[None, :, None, None]
    along_y = speed_y[None, None, :, None]
    carry_x = jnp.where(along_x > 0, along_x * (centre - x_dn), along_x * (x_up - centre))
    behind_y = centre - jnp.roll(centre, 1, 3)
    ahead_y = jnp.roll(centre, -1, 3) - centre
    carry_y = jnp.where(along_y > 0, along_y * behind_y, along_y * ahead_y)
    speed_up = -CONTROL_COST * (control_up - control)
    speed_dn = -CONTROL_COST * (control - control_dn)
    flux_up = jnp.maximum(speed_up, 0.0) * centre + jnp.minimum(speed_up, 0.0) * a_up
    flux_dn = jnp.maximum(speed_dn, 0.0) * a_dn + jnp.minimum(speed_dn, 0.0) * centre
    b_up = along_second(centre, 1)
    b_dn = along_second(centre, -1)
    side_up = -CONTROL_COST * (along_second(control, 1) - control)
    side_dn = -CONTROL_COST * (control - along_second(control, -1))
    flux_right = jnp.maximum(side_up, 0.0) * centre + jnp.minimum(side_up, 0.0) * b_up
    flux_left = jnp.maximum(side_dn, 0.0) * b_dn + jnp.minimum(side_dn, 0.0) * centre
    spread = VISCOSITY * (a_up + a_dn - 2.0 * centre + b_up + b_dn - 2.0 * centre)
    return centre - carry_x - carry_y - (flux_up - flux_dn) - (flux_right - flux_left) + spread


def reference(value_next, density):
    grid_v = value_next.shape[1]
    mass = jnp.sum(density, axis=(1, 2)) / (grid_v * grid_v)
    crowding = CROWDING * mass * mass
    speed_all = speeds(0, grid_v, grid_v)
    pieces = []
    for offset in range(0, grid_v, 8):
        rows = offset + jnp.arange(8, dtype=jnp.int32)
        upper = jnp.minimum(rows + 1, grid_v - 1).astype(jnp.int32)
        lower = jnp.maximum(rows - 1, 0).astype(jnp.int32)
        centre = value_next[:, offset:offset + 8]
        pieces.append(value_core(centre, jnp.roll(centre, -1, 0), jnp.roll(centre, 1, 0),
                                 jnp.take(value_next, upper, axis=1), jnp.take(value_next, lower, axis=1),
                                 speed_all[offset:offset + 8], speed_all, crowding))
    value_now = jnp.concatenate(pieces, 1)
    parts = []
    for offset in range(0, grid_v, 8):
        rows = offset + jnp.arange(8, dtype=jnp.int32)
        upper = jnp.minimum(rows + 1, grid_v - 1).astype(jnp.int32)
        lower = jnp.maximum(rows - 1, 0).astype(jnp.int32)
        centre = density[:, offset:offset + 8]
        parts.append(density_core(centre, jnp.roll(centre, -1, 0), jnp.roll(centre, 1, 0),
                                  jnp.take(density, upper, axis=1), jnp.take(density, lower, axis=1),
                                  value_now[:, offset:offset + 8], jnp.take(value_now, upper, axis=1),
                                  jnp.take(value_now, lower, axis=1), speed_all[offset:offset + 8], speed_all))
    density_next = jnp.concatenate(parts, 1)
    return value_now, density_next
```

```python
import jax
import jax.numpy as jnp
from jax import lax
from jax.experimental import pallas as pl
from jax.experimental.pallas import tpu as pltpu
from jax.sharding import PartitionSpec as P

COURANT = 0.4
CONTROL_COST = 0.25
VISCOSITY = 0.15
CROWDING = 0.3
LANES = 128


def make_kernel(vels, slabs, rows, grid_v, cells, axes):
    blocks = cells // LANES
    half = grid_v // 2
    inner = rows - 1

    def device(vel, pos):
        place = {"vel": vel, "pos": pos}
        return tuple(place[name] for name in axes)

    def remote(src, dst, send, recv, target):
        return pltpu.make_async_remote_copy(
            src_ref=src,
            dst_ref=dst,
            send_sem=send,
            recv_sem=recv,
            device_id=target,
            device_id_type=pl.DeviceIdType.MESH,
        )

    def kernel(
        value, density, now, nxt,
        val, den, val_x, den_x, val_h, den_h, now_h, mass, crowd, slope,
        load_sem, x_send, x_recv, h_send, h_recv, n_send, n_recv, m_send, m_recv,
    ):
        vel = lax.axis_index("vel")
        pos = lax.axis_index("pos")
        rising = (vel >= vels // 2).astype(jnp.int32)
        after = lax.rem(pos + 1, slabs)
        before = lax.rem(pos + slabs - 1, slabs)
        val_to = jnp.where(rising == 1, before, after)
        den_to = jnp.where(rising == 1, after, before)
        near = 1 - rising
        far = rising

        load_den = pltpu.make_async_copy(density, den, load_sem.at[0])
        load_val = pltpu.make_async_copy(value, val, load_sem.at[1])
        load_den.start()
        load_val.start()

        barrier = pltpu.get_barrier_semaphore()
        pl.semaphore_signal(barrier, 1, device_id=device(vel, after), device_id_type=pl.DeviceIdType.MESH)
        pl.semaphore_signal(barrier, 1, device_id=device(vel, before), device_id_type=pl.DeviceIdType.MESH)
        for step in range(1, vels):
            pl.semaphore_signal(
                barrier, 1, device_id=device(lax.rem(vel + step, vels), pos),
                device_id_type=pl.DeviceIdType.MESH,
            )
        pl.semaphore_wait(barrier, vels + 1)

        def x_copies(a):
            return (
                remote(value.at[near, a], val_x.at[a], x_send.at[0, a], x_recv.at[0, a], device(vel, val_to)),
                remote(density.at[far, a], den_x.at[a], x_send.at[1, a], x_recv.at[1, a], device(vel, den_to)),
            )

        def start_x(a):
            for copy in x_copies(a):
                copy.start()

        start_x(0)
        start_x(rows - 1)

        upward = device(jnp.minimum(vel + 1, vels - 1), pos)
        downward = device(jnp.maximum(vel - 1, 0), pos)

        def h_copies(which):
            array, held = ((value, val_h), (density, den_h))[which]
            return (
                remote(array.at[:, rows - 1], held.at[0], h_send.at[which, 0], h_recv.at[which, 0], upward),
                remote(array.at[:, 0], held.at[1], h_send.at[which, 1], h_recv.at[which, 1], downward),
            )

        def start_middle(a, carry):
            start_x(a)
            return carry

        lax.fori_loop(1, rows - 1, start_middle, 0)

        index = lax.broadcasted_iota(jnp.int32, (grid_v, LANES), 0).astype(jnp.float32)
        slope[...] = jnp.abs(COURANT * ((index + 0.5 - grid_v / 2) / (grid_v / 2)))

        load_den.wait()
        for i in range(2):
            def add_row(a, total):
                row = den[i, a]
                for k in range(grid_v // 8):
                    total = total + row[8 * k:8 * k + 8]
                return total

            total = lax.fori_loop(0, rows, add_row, jnp.zeros((8, cells), jnp.float32))
            mass[vel, pl.ds(i, 1)] = jnp.sum(total, axis=0, keepdims=True)

        def m_copy(step):
            return remote(
                mass.at[vel], mass.at[vel], m_send.at[step - 1], m_recv.at[step - 1],
                device(lax.rem(vel + step, vels), pos),
            )

        for step in range(1, vels):
            m_copy(step).start()
        for which in (0, 1):
            up, down = h_copies(which)
            pl.when(vel < vels - 1)(up.start)
            pl.when(vel > 0)(down.start)
        load_val.wait()
        for step in range(1, vels):
            m_copy(step).wait_recv()
        for i in range(2):
            whole = mass[0, pl.ds(i, 1)]
            for group in range(1, vels):
                whole = whole + mass[group, pl.ds(i, 1)]
            whole = whole / (grid_v * grid_v)
            crowd[i] = jnp.broadcast_to(CROWDING * whole * whole, (8, cells))

        place_b = lax.broadcasted_iota(jnp.int32, (grid_v, LANES), 0)
        first_b = place_b == 0
        last_b = place_b == grid_v - 1
        lane = lax.broadcasted_iota(jnp.int32, (half, LANES), 1)

        def speed(a):
            place = (vel * rows + a).astype(jnp.float32)
            return jnp.abs(COURANT * ((place + 0.5 - grid_v / 2) / (grid_v / 2)))

        def cut(block):
            return pl.ds((block % blocks) * LANES, LANES)

        def shifted(ref, i, a, block, lower_step):
            def part(start, step):
                here = ref[i, a, pl.ds(start, half), cut(block)]
                there = ref[i, a, pl.ds(start, half), cut(block + step)]
                amount = LANES - 1 if step > 0 else 1
                edge = LANES - 1 if step > 0 else 0
                return jnp.where(lane == edge, pltpu.roll(there, amount, 1), pltpu.roll(here, amount, 1))

            return jnp.concatenate([part(0, lower_step), part(half, -lower_step)], 0)

        def value_row(i, a, x_row, up_row, down_row):
            pace = speed(a)
            for block in range(blocks):
                centre = val[i, a, :, cut(block)]
                upper = up_row(block, centre) - centre
                lower = centre - down_row(block, centre)
                side = jnp.where(last_b, 0.0, pltpu.roll(centre, grid_v - 1, 0) - centre)
                back = jnp.where(first_b, 0.0, pltpu.roll(side, 1, 0))
                bend = (
                    jnp.square(jnp.maximum(lower, 0.0))
                    + jnp.square(jnp.minimum(upper, 0.0))
                    + jnp.square(jnp.maximum(back, 0.0))
                    + jnp.square(jnp.minimum(side, 0.0))
                )
                crowding = jnp.concatenate([crowd[i, :, cut(block)]] * (grid_v // 8), 0)
                now[i, a, :, cut(block)] = (
                    centre
                    + pace * (x_row(block) - centre)
                    + slope[...] * (shifted(val, i, a, block, -1) - centre)
                    - (0.5 * CONTROL_COST) * bend
                    + VISCOSITY * (upper - lower + side - back)
                    + crowding
                )

        def density_row(i, a, x_row, up_row, down_row, up_now, down_now):
            pace = speed(a)
            for block in range(blocks):
                centre = den[i, a, :, cut(block)]
                control = now[i, a, :, cut(block)]
                above = up_row(block, centre)
                below = down_row(block, centre)
                rise = -CONTROL_COST * (up_now(block, control) - control)
                fall = -CONTROL_COST * (control - down_now(block, control))
                flux_up = jnp.maximum(rise, 0.0) * centre + jnp.minimum(rise, 0.0) * above
                flux_dn = jnp.maximum(fall, 0.0) * below + jnp.minimum(fall, 0.0) * centre
                right = pltpu.roll(centre, grid_v - 1, 0)
                turn = -CONTROL_COST * (pltpu.roll(control, grid_v - 1, 0) - control)
                flux_side = jnp.maximum(turn, 0.0) * centre + jnp.minimum(turn, 0.0) * right
                flux_side = jnp.where(last_b, 0.0, flux_side - VISCOSITY * (right - centre))
                flux_back = jnp.where(first_b, 0.0, pltpu.roll(flux_side, 1, 0))
                nxt[i, a, :, cut(block)] = (
                    centre
                    + pace * (x_row(block) - centre)
                    + slope[...] * (shifted(den, i, a, block, 1) - centre)
                    - (flux_up - flux_dn)
                    - (flux_side - flux_back)
                    + VISCOSITY * (above + below - 2.0 * centre)
                )

        def row_of(ref, i, a):
            return lambda block, centre=None: ref[i, a, :, cut(block)]

        def line_of(ref, a):
            return lambda block: ref[a, :, cut(block)]

        def edge_of(ref, side, i):
            clamp = vel == (0 if side == 0 else vels - 1)
            return lambda block, centre: jnp.where(clamp, centre, ref[side, i, :, cut(block)])

        def neighbours(ref, held, i, a, kind):
            up = edge_of(held, 1, i) if kind == "last" else row_of(ref, i, a + 1)
            down = edge_of(held, 0, i) if kind == "first" else row_of(ref, i, a - 1)
            return up, down

        def near_value(a, kind="middle"):
            value_row(near, a, row_of(val, far, a), *neighbours(val, val_h, near, a, kind))

        def far_value(a, kind="middle"):
            value_row(far, a, line_of(val_x, a), *neighbours(val, val_h, far, a, kind))

        def near_density(a, kind="middle"):
            density_row(
                near, a, line_of(den_x, a), *neighbours(den, den_h, near, a, kind),
                *neighbours(now, now_h, near, a, kind),
            )

        def far_density(a, kind="middle"):
            density_row(
                far, a, row_of(den, near, a), *neighbours(den, den_h, far, a, kind),
                *neighbours(now, now_h, far, a, kind),
            )

        def n_copies(i):
            return (
                remote(now.at[i, rows - 1], now_h.at[0, i], n_send.at[0, i], n_recv.at[0, i], upward),
                remote(now.at[i, 0], now_h.at[1, i], n_send.at[1, i], n_recv.at[1, i], downward),
            )

        def send_now(i):
            up, down = n_copies(i)
            pl.when(vel < vels - 1)(up.start)
            pl.when(vel > 0)(down.start)

        def loop(start, stop, step):
            def one(a, carry):
                step(a)
                return carry

            lax.fori_loop(start, stop, one, 0)

        def wait_x(which, a):
            x_copies(a)[which].wait_recv()

        def arrive(copies):
            up, down = copies
            pl.when(vel > 0)(up.wait_recv)
            pl.when(vel < vels - 1)(down.wait_recv)

        def advance(a):
            wait_x(0, a)
            far_value(a)

        def settle(a):
            advance(a)
            far_density(a - 1)
            wait_x(1, a)
            near_density(a)

        loop(1, rows - 1, near_value)
        loop(1, 3, advance)
        wait_x(1, 1)
        wait_x(1, 2)
        near_density(2)
        loop(3, 6, settle)
        arrive(h_copies(0))
        near_value(0, "first")
        near_value(rows - 1, "last")
        send_now(near)
        wait_x(0, 0)
        wait_x(0, rows - 1)
        far_value(0, "first")
        far_value(rows - 1, "last")
        send_now(far)
        loop(6, 12, settle)
        arrive(h_copies(1))
        for i in range(2):
            arrive(n_copies(i))
        near_density(1)
        far_density(1)
        wait_x(1, 0)
        near_density(0, "first")
        far_density(0, "first")
        wait_x(1, rows - 1)
        near_density(rows - 1, "last")
        loop(12, rows - 1, settle)
        far_density(rows - 2)
        far_density(rows - 1, "last")

        def drain(a):
            for copy in x_copies(a):
                copy.wait_send()

        loop(0, rows, drain)
        for which in (0, 1):
            up, down = h_copies(which)
            pl.when(vel < vels - 1)(up.wait_send)
            pl.when(vel > 0)(down.wait_send)
            up, down = n_copies(which)
            pl.when(vel < vels - 1)(up.wait_send)
            pl.when(vel > 0)(down.wait_send)
        for step in range(1, vels):
            m_copy(step).wait_send()

    return kernel


def solution(mesh):
    axes = mesh.axis_names
    vels, slabs = mesh.shape["vel"], mesh.shape["pos"]

    def body(value_next, density):
        depth, rows, grid_v, cells = value_next.shape
        line = (grid_v, cells)
        f32 = jnp.float32
        anywhere = pl.BlockSpec(memory_space=pltpu.HBM)
        held = pl.BlockSpec(memory_space=pltpu.VMEM)
        dma = pltpu.SemaphoreType.DMA
        return pl.pallas_call(
            make_kernel(vels, slabs, rows, grid_v, cells, axes),
            name="game_step",
            out_shape=(jax.ShapeDtypeStruct(value_next.shape, f32),) * 2,
            in_specs=[anywhere, anywhere],
            out_specs=(held, held),
            scratch_shapes=[
                pltpu.VMEM(value_next.shape, f32),
                pltpu.VMEM(value_next.shape, f32),
                pltpu.VMEM((rows,) + line, f32),
                pltpu.VMEM((rows,) + line, f32),
                pltpu.VMEM((2, depth) + line, f32),
                pltpu.VMEM((2, depth) + line, f32),
                pltpu.VMEM((2, depth) + line, f32),
                pltpu.VMEM((vels, 8, cells), f32),
                pltpu.VMEM((depth, 8, cells), f32),
                pltpu.VMEM((grid_v, LANES), f32),
                dma((2,)),
                dma((2, rows)),
                dma((2, rows)),
                dma((2, 2)),
                dma((2, 2)),
                dma((2, 2)),
                dma((2, 2)),
                dma((vels - 1,)),
                dma((vels - 1,)),
            ],
            compiler_params=pltpu.CompilerParams(
                collective_id=0, has_side_effects=True, vmem_limit_bytes=44 << 20
            ),
        )(value_next, density)

    spec = P("pos", "vel", None, None)
    return jax.shard_map(body, mesh=mesh, in_specs=(spec, spec), out_specs=(spec, spec), check_vma=False)
```
